32 devices in a mesh: tm: 8 (over z, y), stream: 4 (over x, core).
Axes of the slice: x: 2, y: 2, z: 4, core: 2. Of those that a mesh axis runs over, the one named last changes fastest.
Arguments:
- signal: bfloat16 [4, 49152, 256], P('stream', 'tm'), may hold values from -6 to 6
- lengths: int32 [4], P('stream'), may hold values from 12288 to 49152, as said below
- w_conv: bfloat16 [512, 512], replicated, may hold values from -0.25 to 0.25
- w_res: bfloat16 [256, 256], replicated, may hold values from -0.375 to 0.375
- w_in: bfloat16 [256, 1024], replicated, may hold values from -0.375 to 0.375
- w_qkv: bfloat16 [1024, 3072], P(None, 'stream')
- w_out: bfloat16 [1024, 1024], P('stream'), may hold values from -0.1875 to 0.1875
- d_out: bfloat16 [4, 192, 1024], P('stream', 'tm'), may hold values from -6 to 6
Outputs:
- out: bfloat16 [4, 192, 1024], P('stream', 'tm')
- d_signal: bfloat16 [4, 49152, 256], P('stream', 'tm')
- g_conv: float32 [512, 512], P('stream')
- g_res: float32 [256, 256], P('stream')
- g_in: float32 [256, 1024], P('stream')
- g_qkv: float32 [1024, 3072], P('tm', 'stream')
- g_out: float32 [1024, 1024], P('stream', 'tm')
The draws below stay inside these ranges and needn't reach their ends.
Inputs may be any that keep to these rules, and one draw needn't show every extreme that they name: `lengths`: some stay has all 49152 samples valid and some other stay exactly 12288.
All inputs are finite; a program needn't handle non-finite values.
Results may differ from the reference program's by a relative error of at most 0.013.
Values may be sent and summed in bfloat16 or wider, within the bound.
A program may use at most 128 MiB of HBM per device.

```python
import math
import jax
import jax.numpy as jnp
from jax import lax

CONV_CHANNELS = 256
D = 1024
HEADS = 16
HEAD = 64
POOL = 256
DILATION_STEP = 512
STAYS = 4
STAY_SAMPLES = 49152
TOKENS = 192


def draw_lengths(key, part):
    values = jax.random.randint(key, (STAYS,), STAY_SAMPLES // 4, STAY_SAMPLES + 1)
    where_full = jax.random.randint(jax.random.fold_in(key, 11), (), 0, STAYS)
    where_short = (where_full + 1) % STAYS
    places = jnp.arange(STAYS)
    values = jnp.where(places == where_full, STAY_SAMPLES, values)
    values = jnp.where(places == where_short, STAY_SAMPLES // 4, values)
    return values.astype(jnp.int32)


def draw_w_qkv(key, part):
    base = jax.random.normal(key, (D, HEADS, 3, D // HEADS), jnp.float32) / math.sqrt(D)
    return base.reshape(D, 3 * D).astype(jnp.bfloat16)


def block_scale(own_key, extent, pieces, low, high):
    loudness, own = 1.0, jax.random.fold_in(own_key, 6)
    for dim, shards_of in pieces:
        draws = jnp.exp(jax.random.uniform(jax.random.fold_in(own, dim), (shards_of,), jnp.float32, low / len(pieces), high / len(pieces)))
        loudness = loudness * jnp.repeat(draws, extent[dim] // shards_of).reshape([-1 if axis == dim else 1 for axis in range(len(extent))])
    return loudness


def scatter_about(own_key, shape, spread, bound, split=(), held_as=jnp.bfloat16):
    level = block_scale(own_key, shape, split, -0.22, 0.18) if split else 1.0
    values = jax.random.normal(own_key, shape, jnp.float32) * spread * level
    return jnp.minimum(jnp.maximum(values, -bound), bound).astype(held_as)


def setup_inputs(seed: int = 0) -> dict:
    key_of = jax.random.split(jax.random.key(seed), 9)
    return {
        "signal": scatter_about(key_of[0], (STAYS, STAY_SAMPLES, CONV_CHANNELS), 1.0, 6.0, ((0, 4), (1, 8))),
        "lengths": draw_lengths(jax.random.fold_in(key_of[8], 71), 0),
        "w_conv": scatter_about(key_of[2], (2 * CONV_CHANNELS, 2 * CONV_CHANNELS), (2 * CONV_CHANNELS) ** -0.5, 0.25),
        "w_res": scatter_about(key_of[3], (CONV_CHANNELS, CONV_CHANNELS), CONV_CHANNELS ** -0.5, 0.375),
        "w_in": scatter_about(key_of[4], (CONV_CHANNELS, D), CONV_CHANNELS ** -0.5, 0.375),
        "w_qkv": draw_w_qkv(jax.random.fold_in(key_of[8], 71), 0),
        "w_out": scatter_about(key_of[6], (D, D), D ** -0.5, 0.1875, ((0, 4),)),
        "d_out": scatter_about(key_of[7], (STAYS, TOKENS, D), 1.0, 6.0, ((0, 4), (1, 8))),
    }


EPS = 1e-05
HIGH = lax.Precision.HIGHEST

def conv_parts(stay_signal_rows, length, w_conv):
    past_rows = jnp.concatenate([jnp.zeros((DILATION_STEP, CONV_CHANNELS), stay_signal_rows.dtype), stay_signal_rows[:STAY_SAMPLES - DILATION_STEP]], axis=0)
    joined = jnp.concatenate([past_rows, stay_signal_rows], axis=1)
    mixed = jnp.dot(joined, w_conv, preferred_element_type=jnp.float32)
    tanh_f = jnp.tanh(mixed[:, :CONV_CHANNELS])
    sig_g = jax.nn.sigmoid(mixed[:, CONV_CHANNELS:])
    hidden = (tanh_f * sig_g).astype(jnp.bfloat16)
    valid = (jnp.arange(STAY_SAMPLES) < length)[:, None]
    return (joined, tanh_f, sig_g, hidden, valid)

def reference(signal, lengths, w_conv, w_res, w_in, w_qkv, w_out, d_out):

    def stay_forward(pair):
        stay_signal_rows, length = pair
        joined, tanh_f, sig_g, hidden, valid = conv_parts(stay_signal_rows, length, w_conv)
        resid = jnp.where(valid, stay_signal_rows.astype(jnp.float32) + jnp.dot(hidden, w_res, preferred_element_type=jnp.float32), 0.0)
        return lax.optimization_barrier(jnp.mean(resid.reshape(TOKENS, POOL, CONV_CHANNELS), axis=1)).astype(jnp.bfloat16)
    pooled = lax.map(stay_forward, (signal, lengths))
    pooled_flat = pooled.reshape(STAYS * TOKENS, CONV_CHANNELS)
    tokens = jnp.dot(pooled_flat, w_in, preferred_element_type=jnp.float32).astype(jnp.bfloat16)
    tok_values = tokens.astype(jnp.float32)
    tok_scale = lax.rsqrt(lax.optimization_barrier(jnp.mean(tok_values * tok_values, axis=-1, keepdims=True)) + EPS)
    normed = (tok_values * tok_scale).astype(jnp.bfloat16)
    proj = jnp.dot(normed, w_qkv, preferred_element_type=jnp.float32).astype(jnp.bfloat16)
    proj = proj.reshape(STAYS, TOKENS, HEADS, 3, HEAD).astype(jnp.float32)
    query = proj[:, :, :, 0]
    keys = proj[:, :, :, 1]
    values = proj[:, :, :, 2]
    scale = 1.0 / math.sqrt(HEAD)
    position = jnp.arange(TOKENS)
    allowed = (position[None, None, :] <= position[None, :, None]) & ((position * POOL)[None, None, :] < lengths[:, None, None])
    scores = jnp.einsum('sqhe,skhe->shqk', query, keys, precision=HIGH) * scale
    scores = jnp.where(allowed[:, None], scores, -1e+30)
    top = lax.optimization_barrier(jnp.max(scores, axis=-1, keepdims=True))
    weights = jnp.exp(scores - top)
    prob = weights / lax.optimization_barrier(jnp.sum(weights, axis=-1, keepdims=True))
    prob16 = prob.astype(jnp.bfloat16).astype(jnp.float32)
    context = jnp.einsum('shqk,skhe->sqhe', prob16, values, precision=HIGH).astype(jnp.bfloat16)
    context = context.reshape(STAYS * TOKENS, D)
    part = jnp.dot(context, w_out, preferred_element_type=jnp.float32)
    out = (tok_values + part).astype(jnp.bfloat16).reshape(STAYS, TOKENS, D)
    grad_flat = d_out.reshape(STAYS * TOKENS, D)
    g_out = jnp.dot(context.T, grad_flat, preferred_element_type=jnp.float32)
    d_context = jnp.dot(grad_flat, w_out.T, preferred_element_type=jnp.float32).astype(jnp.bfloat16)
    d_context = d_context.reshape(STAYS, TOKENS, HEADS, HEAD).astype(jnp.float32)
    d_prob = jnp.einsum('sqhe,skhe->shqk', d_context, values, precision=HIGH)
    d_score = prob * (d_prob - lax.optimization_barrier(jnp.sum(d_prob * prob, axis=-1, keepdims=True)))
    d_query = scale * jnp.einsum('shqk,skhe->sqhe', d_score, keys, precision=HIGH)
    d_keys = scale * jnp.einsum('shqk,sqhe->skhe', d_score, query, precision=HIGH)
    d_values = jnp.einsum('shqk,sqhe->skhe', prob16, d_context, precision=HIGH)
    d_proj = jnp.stack([d_query, d_keys, d_values], axis=3).reshape(STAYS * TOKENS, 3 * D)
    g_qkv = jnp.dot(normed.astype(jnp.float32).T, d_proj, precision=HIGH)
    d_normed = jnp.dot(d_proj, w_qkv.astype(jnp.float32).T, precision=HIGH)
    inner = lax.optimization_barrier(jnp.sum(d_normed * tok_values, axis=-1, keepdims=True))
    cube = tok_scale * tok_scale * tok_scale
    d_tokens = grad_flat.astype(jnp.float32) + tok_scale * d_normed - tok_values * cube * inner / D
    g_in = jnp.dot(pooled_flat.astype(jnp.float32).T, d_tokens, precision=HIGH)
    d_pooled = jnp.dot(d_tokens, w_in.astype(jnp.float32).T, precision=HIGH).reshape(STAYS, TOKENS, CONV_CHANNELS)

    def stay_backward(triple):
        stay_signal_rows, length, d_pool = triple
        joined, tanh_f, sig_g, hidden, valid = conv_parts(stay_signal_rows, length, w_conv)
        d_resid = jnp.where(valid, jnp.repeat(d_pool / POOL, POOL, axis=0), 0.0).astype(jnp.bfloat16)
        res_grad = jnp.dot(hidden.T, d_resid, preferred_element_type=jnp.float32)
        d_hidden = jnp.dot(d_resid, w_res.T, preferred_element_type=jnp.float32)
        d_mixed = jnp.concatenate([d_hidden * (1.0 - tanh_f * tanh_f) * sig_g, d_hidden * tanh_f * sig_g * (1.0 - sig_g)], axis=1).astype(jnp.bfloat16)
        conv_grad = jnp.dot(joined.T, d_mixed, preferred_element_type=jnp.float32)
        d_joined = jnp.dot(d_mixed, w_conv.T, preferred_element_type=jnp.float32)
        past_gradient = d_joined[:, :CONV_CHANNELS].astype(jnp.bfloat16)
        later_gradient = jnp.concatenate([past_gradient[DILATION_STEP:], jnp.zeros((DILATION_STEP, CONV_CHANNELS), past_gradient.dtype)], axis=0)
        d_stay = (d_resid.astype(jnp.float32) + d_joined[:, CONV_CHANNELS:] + later_gradient.astype(jnp.float32)).astype(jnp.bfloat16)
        return (d_stay, conv_grad, res_grad)
    d_signal, conv_grads, res_grads = lax.map(stay_backward, (signal, lengths, d_pooled))
    return (out, d_signal, lax.optimization_barrier(jnp.sum(conv_grads, axis=0)), lax.optimization_barrier(jnp.sum(res_grads, axis=0)), g_in, g_qkv, g_out)
```

```python
import functools
import math

import jax
import jax.numpy as jnp
from jax import lax
from jax.experimental import pallas as pl
from jax.experimental.pallas import tpu as pltpu
from jax.sharding import PartitionSpec as P

HEADS = 16
POOL = 256
DILATION_STEP = 512
EPS = 1e-05
BF16 = jnp.bfloat16
F32 = jnp.float32
MESH = pl.DeviceIdType.MESH
VMEM_SPEC = pl.BlockSpec(memory_space=pltpu.VMEM)


def dot(eq, a, b):
    return jnp.einsum(eq, a, b, preferred_element_type=F32)


def exchange_kernel(axis, n, kinds, *refs):
    k = len(kinds)
    ins, outs = refs[:k], refs[k : 2 * k]
    rest = list(refs[2 * k :])
    slots = [rest.pop(0) if kind == "reduce" else None for kind in kinds]
    send, recv, local_sem = rest
    me = lax.axis_index(axis)
    barrier = pltpu.get_barrier_semaphore()
    for d in range(1, n):
        pl.semaphore_signal(
            barrier, inc=1, device_id={axis: lax.rem(me + d, n)}, device_id_type=MESH
        )
    pl.semaphore_wait(barrier, n - 1)
    copies = []
    locals_ = []
    for j, kind in enumerate(kinds):
        for d in range(1, n):
            peer = lax.rem(me + d, n)
            src = ins[j] if kind.startswith("gather") else ins[j].at[peer]
            if kind == "reduce":
                dst = slots[j].at[d - 1]
            elif kind.endswith("1"):
                dst = outs[j].at[:, me]
            else:
                dst = outs[j].at[me]
            copy = pltpu.make_async_remote_copy(
                src_ref=src,
                dst_ref=dst,
                send_sem=send.at[j, d - 1],
                recv_sem=recv.at[j, d - 1],
                device_id={axis: peer},
                device_id_type=MESH,
            )
            copy.start()
            copies.append(copy)
        if kind != "reduce":
            src = ins[j] if kind.startswith("gather") else ins[j].at[me]
            dst = outs[j].at[:, me] if kind.endswith("1") else outs[j].at[me]
            copy = pltpu.make_async_copy(src, dst, local_sem.at[j])
            copy.start()
            locals_.append(copy)
    for copy in locals_:
        copy.wait()
    for copy in copies:
        copy.wait()
    for j, kind in enumerate(kinds):
        if kind == "reduce":
            total = ins[j][me].astype(F32)
            for d in range(1, n):
                total += slots[j][d - 1].astype(F32)
            outs[j][...] = total


def exchange(axis, collective, items):
    n = lax.axis_size(axis)
    kinds = tuple(kind for kind, _ in items)
    arrays = [array for _, array in items]
    shapes, slots = [], []
    for kind, array in items:
        inner = array.shape if kind.startswith("gather") else array.shape[1:]
        if kind == "reduce":
            shapes.append(jax.ShapeDtypeStruct(inner, F32))
            slots.append(pltpu.VMEM((n - 1,) + inner, array.dtype))
        elif kind.endswith("1"):
            shapes.append(jax.ShapeDtypeStruct((inner[0], n) + inner[1:], array.dtype))
        else:
            shapes.append(jax.ShapeDtypeStruct((n,) + inner, array.dtype))
    k = len(items)
    return pl.pallas_call(
        functools.partial(exchange_kernel, axis, n, kinds),
        out_shape=shapes,
        in_specs=[VMEM_SPEC] * k,
        out_specs=[VMEM_SPEC] * k,
        scratch_shapes=slots
        + [
            pltpu.SemaphoreType.DMA((k, n - 1)),
            pltpu.SemaphoreType.DMA((k, n - 1)),
            pltpu.SemaphoreType.DMA((k,)),
        ],
        compiler_params=pltpu.CompilerParams(collective_id=collective, has_side_effects=True),
        name=f"exchange_{axis}_{collective}",
    )(*arrays)


def attention_kernel(heads, size, scale, len_ref, proj_ref, dctx_ref, ctx_ref, dproj_ref):
    stay = pl.program_id(0)
    total = proj_ref.shape[1]
    length = len_ref[stay]
    row = lax.broadcasted_iota(jnp.int32, (total, total), 0)
    col = lax.broadcasted_iota(jnp.int32, (total, total), 1)
    allowed = (col <= row) & (col * POOL < length)
    nt = (((1,), (1,)), ((), ()))
    tn = (((0,), (0,)), ((), ()))
    for h in range(heads):
        base = h * 3 * size
        query = proj_ref[0, :, base : base + size]
        key = proj_ref[0, :, base + size : base + 2 * size]
        value = proj_ref[0, :, base + 2 * size : base + 3 * size]
        dctx = dctx_ref[0, :, h * size : (h + 1) * size]
        scores = lax.dot_general(query, key, nt, preferred_element_type=F32) * scale
        scores = jnp.where(allowed, scores, -1e30)
        top = jnp.max(scores, axis=-1, keepdims=True)
        weights = jnp.exp(scores - top)
        prob = weights / jnp.sum(weights, axis=-1, keepdims=True)
        prob16 = prob.astype(BF16)
        context = jnp.dot(prob16, value, preferred_element_type=F32)
        ctx_ref[0, :, h * size : (h + 1) * size] = context.astype(BF16)
        d_prob = lax.dot_general(dctx, value, nt, preferred_element_type=F32)
        d_score = prob * (d_prob - jnp.sum(d_prob * prob, axis=-1, keepdims=True))
        d16 = d_score.astype(BF16)
        d_query = scale * jnp.dot(d16, key, preferred_element_type=F32)
        d_key = scale * lax.dot_general(d16, query, tn, preferred_element_type=F32)
        d_value = lax.dot_general(prob16, dctx, tn, preferred_element_type=F32)
        dproj_ref[0, :, base : base + size] = d_query.astype(BF16)
        dproj_ref[0, :, base + size : base + 2 * size] = d_key.astype(BF16)
        dproj_ref[0, :, base + 2 * size : base + 3 * size] = d_value.astype(BF16)


def attention(proj, d_context, group_len, heads, size):
    group, total, width = proj.shape
    inner = heads * size
    wide = pl.BlockSpec((1, total, width), lambda s: (s, 0, 0))
    thin = pl.BlockSpec((1, total, inner), lambda s: (s, 0, 0))
    return pl.pallas_call(
        functools.partial(attention_kernel, heads, size, 1.0 / math.sqrt(size)),
        grid=(group,),
        out_shape=(
            jax.ShapeDtypeStruct((group, total, inner), BF16),
            jax.ShapeDtypeStruct((group, total, width), BF16),
        ),
        in_specs=[pl.BlockSpec(memory_space=pltpu.SMEM), wide, thin],
        out_specs=(thin, wide),
        name="attention",
    )(group_len, proj, d_context)


def shifted(value, axis, by):
    length = lax.axis_size(axis)
    pairs = [(i, i + by) for i in range(length) if 0 <= i + by < length]
    return lax.ppermute(value, axis, pairs)


def local(signal, lengths, w_conv, w_res, w_in, w_qkv, w_out, d_out):
    stays, samples, chans = signal.shape
    width = w_in.shape[1]
    size = width // HEADS
    heads = w_out.shape[0] // size
    toks = samples // POOL
    tms, parts = lax.axis_size("tm"), lax.axis_size("stream")
    tm = lax.axis_index("tm")
    group = stays * parts
    total = toks * tms
    incoming = shifted(signal[:, samples - DILATION_STEP :], "tm", 1)
    past = jnp.concatenate([incoming, signal[:, : samples - DILATION_STEP]], axis=1)
    joined = jnp.concatenate([past, signal], axis=2)
    mixed = dot("bsc,cd->bsd", joined, w_conv)
    tanh_f = jnp.tanh(mixed[..., :chans])
    sig_g = jax.nn.sigmoid(mixed[..., chans:])
    hidden = (tanh_f * sig_g).astype(BF16)
    pos = tm * samples + jnp.arange(samples, dtype=jnp.int32)
    valid = (pos[None, :] < lengths[:, None])[..., None]
    resid = jnp.where(valid, signal.astype(F32) + dot("bsc,cd->bsd", hidden, w_res), 0.0)
    pooled = jnp.mean(resid.reshape(stays, toks, POOL, chans), axis=2).astype(BF16)
    own_tok = dot("btc,cd->btd", pooled, w_in).astype(BF16)
    lens8 = jnp.broadcast_to(lengths.reshape(stays, 1, 1), (stays, 8, 128))
    g_pool, g_dout, g_len = exchange(
        "stream", 0, [("gather", pooled), ("gather", d_out), ("gather", lens8)]
    )
    group_pool = g_pool.reshape(group, toks, chans)
    group_grad = g_dout.reshape(group, toks, width)
    group_len = g_len.reshape(group, 8, 128)[:, 0, 0]
    d_ctx = dot("btd,ed->bte", group_grad, w_out).astype(BF16)
    columns = width // tms
    grad_cols = group_grad.reshape(group, toks, tms, columns).transpose(2, 0, 1, 3)
    all_pool, all_ctx, all_cols = exchange(
        "tm", 1, [("gather1", group_pool), ("gather1", d_ctx), ("scatter1", grad_cols)]
    )
    all_pool = all_pool.reshape(group, total, chans)
    all_ctx = all_ctx.reshape(group, total, heads * size)
    all_cols = all_cols.reshape(group, total, columns)
    tok = dot("btc,cd->btd", all_pool, w_in).astype(BF16).astype(F32)
    r = lax.rsqrt(jnp.mean(tok * tok, axis=-1, keepdims=True) + EPS)
    normed = (tok * r).astype(BF16)
    proj = dot("btd,de->bte", normed, w_qkv).astype(BF16)
    context, d_proj = attention(proj, all_ctx, group_len, heads, size)
    own_ctx = lax.dynamic_slice_in_dim(context, tm * toks, toks, 1)
    out_part = dot("bte,ed->btd", own_ctx, w_out).astype(BF16)
    g_out = dot("bte,btd->ed", context, all_cols)
    own_norm = lax.dynamic_slice_in_dim(normed, tm * columns, columns, 2)
    g_qkv = dot("btd,bte->de", own_norm, d_proj)
    d_normed = dot("bte,de->btd", d_proj, w_qkv)
    inner = jnp.sum(d_normed * tok, axis=-1, keepdims=True)
    d_group = (r * d_normed - tok * (r * r * r) * inner / width).astype(BF16)
    own_group = lax.dynamic_slice_in_dim(d_group, tm * toks, toks, 1)
    g_in_part = dot("btc,btd->cd", all_pool, d_group).astype(BF16)
    in_rows = chans // parts
    g_in_cols = dot("btc,btd->cd", all_pool, all_cols)
    stream = lax.axis_index("stream")
    g_in_cols = lax.dynamic_slice_in_dim(g_in_cols, stream * in_rows, in_rows, 0)
    s_out, s_group, s_in = exchange(
        "stream",
        2,
        [
            ("reduce", out_part.reshape(parts, stays, toks, width)),
            ("reduce", own_group.reshape(parts, stays, toks, width)),
            ("reduce", g_in_part.reshape(parts, in_rows, width)),
        ],
    )
    out = (own_tok.astype(F32) + s_out).astype(BF16)
    d_tok = (s_group + d_out.astype(F32)).astype(BF16)
    d_pooled = dot("btd,cd->btc", d_tok, w_in)
    spread = jnp.repeat(d_pooled / POOL, POOL, axis=1)
    d_resid = jnp.where(valid, spread, 0.0).astype(BF16)
    g_res = dot("bsc,bsd->cd", hidden, d_resid)
    d_hidden = dot("bsd,cd->bsc", d_resid, w_res)
    d_mixed = jnp.concatenate(
        [d_hidden * (1.0 - tanh_f * tanh_f) * sig_g, d_hidden * tanh_f * sig_g * (1.0 - sig_g)],
        axis=2,
    ).astype(BF16)
    g_conv = dot("bsc,bsd->cd", joined, d_mixed)
    d_joined = dot("bsd,cd->bsc", d_mixed, w_conv)
    past_grad = d_joined[..., :chans].astype(BF16)
    arriving = shifted(past_grad[:, :DILATION_STEP], "tm", -1)
    later = jnp.concatenate([past_grad[:, DILATION_STEP:], arriving], axis=1)
    d_signal = (d_resid.astype(F32) + d_joined[..., chans:] + later.astype(F32)).astype(BF16)
    s_conv, s_res = exchange(
        "stream",
        3,
        [
            ("reduce", g_conv.astype(BF16).reshape(parts, -1, 2 * chans)),
            ("reduce", g_res.astype(BF16).reshape(parts, -1, chans)),
        ],
    )
    t_conv, t_res = exchange(
        "tm",
        4,
        [
            ("reduce", s_conv.astype(BF16).reshape(tms, -1, 2 * chans)),
            ("reduce", s_res.astype(BF16).reshape(tms, -1, chans)),
        ],
    )
    a_conv, a_res, a_in = exchange(
        "tm",
        5,
        [
            ("gather", t_conv.astype(BF16)),
            ("gather", t_res.astype(BF16)),
            ("gather", g_in_cols.astype(BF16)),
        ],
    )
    sum_conv = a_conv.reshape(2 * chans // parts, 2 * chans).astype(F32)
    sum_res = a_res.reshape(chans // parts, chans).astype(F32)
    sum_in = s_in + a_in.transpose(1, 0, 2).reshape(in_rows, width).astype(F32)
    return (out, d_signal, sum_conv, sum_res, sum_in, g_qkv, g_out)


def solution(mesh):
    in_specs = (
        P("stream", "tm", None),
        P("stream"),
        P(),
        P(),
        P(),
        P(None, "stream"),
        P("stream", None),
        P("stream", "tm", None),
    )
    out_specs = (
        P("stream", "tm", None),
        P("stream", "tm", None),
        P("stream", None),
        P("stream", None),
        P("stream", None),
        P("tm", "stream"),
        P("stream", "tm"),
    )
    return jax.shard_map(local, mesh=mesh, in_specs=in_specs, out_specs=out_specs, check_vma=False)
```

```python
import functools
import math

import jax
import jax.numpy as jnp
from jax import lax
from jax.experimental import pallas as pl
from jax.experimental.pallas import tpu as pltpu
from jax.sharding import PartitionSpec as P

HEADS = 16
POOL = 256
DILATION_STEP = 512
EPS = 1e-05
BF16 = jnp.bfloat16
F32 = jnp.float32
HIGH = lax.Precision.HIGHEST
MESH = pl.DeviceIdType.MESH
VMEM_SPEC = pl.BlockSpec(memory_space=pltpu.VMEM)


def dot(eq, a, b):
    return jnp.einsum(eq, a, b, preferred_element_type=F32)


def exchange_kernel(axis, n, kinds, *refs):
    k = len(kinds)
    ins, outs = refs[:k], refs[k : 2 * k]
    rest = list(refs[2 * k :])
    slots = [rest.pop(0) if kind.startswith("reduce") else None for kind in kinds]
    send, recv, local_sem = rest
    me = lax.axis_index(axis)
    barrier = pltpu.get_barrier_semaphore()
    for d in range(1, n):
        pl.semaphore_signal(
            barrier, inc=1, device_id={axis: lax.rem(me + d, n)}, device_id_type=MESH
        )
    pl.semaphore_wait(barrier, n - 1)
    copies = []
    locals_ = []
    for j, kind in enumerate(kinds):
        for d in range(1, n):
            peer = lax.rem(me + d, n)
            src = ins[j] if kind.startswith("gather") else ins[j].at[peer]
            if kind.startswith("reduce"):
                dst = slots[j].at[d - 1]
            elif kind.endswith("1"):
                dst = outs[j].at[:, me]
            else:
                dst = outs[j].at[me]
            copy = pltpu.make_async_remote_copy(
                src_ref=src,
                dst_ref=dst,
                send_sem=send.at[j, d - 1],
                recv_sem=recv.at[j, d - 1],
                device_id={axis: peer},
                device_id_type=MESH,
            )
            copy.start()
            copies.append(copy)
        if not kind.startswith("reduce"):
            src = ins[j] if kind.startswith("gather") else ins[j].at[me]
            dst = outs[j].at[:, me] if kind.endswith("1") else outs[j].at[me]
            copy = pltpu.make_async_copy(src, dst, local_sem.at[j])
            copy.start()
            locals_.append(copy)
    for copy in locals_:
        copy.wait()
    for copy in copies:
        copy.wait()
    for j, kind in enumerate(kinds):
        if kind.startswith("reduce"):
            total = ins[j][me].astype(F32)
            for d in range(1, n):
                total += slots[j][d - 1].astype(F32)
            outs[j][...] = total.astype(outs[j].dtype)


def exchange(axis, collective, items):
    n = lax.axis_size(axis)
    kinds = tuple(kind for kind, _ in items)
    arrays = [array for _, array in items]
    shapes, slots = [], []
    for kind, array in items:
        inner = array.shape if kind.startswith("gather") else array.shape[1:]
        if kind.startswith("reduce"):
            shapes.append(jax.ShapeDtypeStruct(inner, BF16 if kind == "reduceb" else F32))
            slots.append(pltpu.VMEM((n - 1,) + inner, array.dtype))
        elif kind.endswith("1"):
            shapes.append(jax.ShapeDtypeStruct((inner[0], n) + inner[1:], array.dtype))
        else:
            shapes.append(jax.ShapeDtypeStruct((n,) + inner, array.dtype))
    k = len(items)
    return pl.pallas_call(
        functools.partial(exchange_kernel, axis, n, kinds),
        out_shape=shapes,
        in_specs=[VMEM_SPEC] * k,
        out_specs=[VMEM_SPEC] * k,
        scratch_shapes=slots
        + [
            pltpu.SemaphoreType.DMA((k, n - 1)),
            pltpu.SemaphoreType.DMA((k, n - 1)),
            pltpu.SemaphoreType.DMA((k,)),
        ],
        compiler_params=pltpu.CompilerParams(collective_id=collective, has_side_effects=True),
        name=f"exchange_{axis}_{collective}",
    )(*arrays)


def attention_kernel(heads, size, scale, len_ref, proj_ref, dctx_ref, ctx_ref, dproj_ref):
    stay = pl.program_id(0)
    total = proj_ref.shape[1]
    length = len_ref[stay]
    row = lax.broadcasted_iota(jnp.int32, (total, total), 0)
    col = lax.broadcasted_iota(jnp.int32, (total, total), 1)
    allowed = (col <= row) & (col * POOL < length)
    nt = (((1,), (1,)), ((), ()))
    tn = (((0,), (0,)), ((), ()))
    for h in range(heads):
        base = h * 3 * size
        query = proj_ref[0, :, base : base + size]
        key = proj_ref[0, :, base + size : base + 2 * size]
        value = proj_ref[0, :, base + 2 * size : base + 3 * size]
        dctx = dctx_ref[0, :, h * size : (h + 1) * size]
        scores = lax.dot_general(query, key, nt, preferred_element_type=F32) * scale
        scores = jnp.where(allowed, scores, -1e30)
        top = jnp.max(scores, axis=-1, keepdims=True)
        weights = jnp.exp(scores - top)
        prob = weights / jnp.sum(weights, axis=-1, keepdims=True)
        prob16 = prob.astype(BF16)
        context = jnp.dot(prob16, value, preferred_element_type=F32)
        ctx_ref[0, :, h * size : (h + 1) * size] = context.astype(BF16)
        d_prob = lax.dot_general(dctx, value, nt, preferred_element_type=F32)
        d_score = prob * (d_prob - jnp.sum(d_prob * prob, axis=-1, keepdims=True))
        d16 = d_score.astype(BF16)
        d_query = scale * jnp.dot(d16, key, preferred_element_type=F32)
        d_key = scale * lax.dot_general(d16, query, tn, preferred_element_type=F32)
        d_value = lax.dot_general(prob16, dctx, tn, preferred_element_type=F32)
        dproj_ref[0, :, base : base + size] = d_query.astype(BF16)
        dproj_ref[0, :, base + size : base + 2 * size] = d_key.astype(BF16)
        dproj_ref[0, :, base + 2 * size : base + 3 * size] = d_value.astype(BF16)


def attention(proj, d_context, group_len, heads, size):
    group, total, width = proj.shape
    inner = heads * size
    wide = pl.BlockSpec((1, total, width), lambda s: (s, 0, 0))
    thin = pl.BlockSpec((1, total, inner), lambda s: (s, 0, 0))
    return pl.pallas_call(
        functools.partial(attention_kernel, heads, size, 1.0 / math.sqrt(size)),
        grid=(group,),
        out_shape=(
            jax.ShapeDtypeStruct((group, total, inner), BF16),
            jax.ShapeDtypeStruct((group, total, width), BF16),
        ),
        in_specs=[pl.BlockSpec(memory_space=pltpu.SMEM), wide, thin],
        out_specs=(thin, wide),
        name="attention",
    )(group_len, proj, d_context)


def tile_valid(info_ref, tile, step):
    row = lax.broadcasted_iota(jnp.int32, (tile, 1), 0)
    return info_ref[0] + step * tile + row < info_ref[1]


def joined_tile(first, in_ref, past_ref, cur_ref):
    past = jnp.where(first, in_ref[...], past_ref[...])
    return jnp.concatenate([past, cur_ref[...]], axis=1)


def forward_kernel(info_ref, in_ref, past_ref, cur_ref, w_ref, t_ref, s_ref, hs_ref, ss_ref):
    i = pl.program_id(0)
    tile, chans = cur_ref.shape
    joined = joined_tile(i == 0, in_ref, past_ref, cur_ref)
    mixed = jnp.dot(joined, w_ref[...], preferred_element_type=F32)
    t = jnp.tanh(mixed[:, :chans])
    s = jax.nn.sigmoid(mixed[:, chans:])
    t_ref[...] = t
    s_ref[...] = s
    valid = tile_valid(info_ref, tile, i)
    hidden = jnp.where(valid, (t * s).astype(BF16).astype(F32), 0.0)
    kept = jnp.where(valid, cur_ref[...].astype(F32), 0.0)
    for j in range(tile // POOL):
        rows = slice(j * POOL, (j + 1) * POOL)
        hs_ref[0, j : j + 1, :] = jnp.sum(hidden[rows], axis=0, keepdims=True)
        ss_ref[0, j : j + 1, :] = jnp.sum(kept[rows], axis=0, keepdims=True)


def backward_kernel(
    steps, info_ref, in_ref, past_ref, cur_ref, t_ref, s_ref, dh_ref, dr_ref, w_ref,
    sig_ref, first_ref, g_ref, acc_ref, later_ref,
):
    i = pl.program_id(0)
    step = steps - 1 - i
    tile, chans = cur_ref.shape

    @pl.when(i == 0)
    def _():
        acc_ref[...] = jnp.zeros_like(acc_ref)
        later_ref[...] = jnp.zeros_like(later_ref)

    joined = joined_tile(step == 0, in_ref, past_ref, cur_ref)
    valid = tile_valid(info_ref, tile, step)

    def spread(ref):
        pieces = [
            jnp.broadcast_to(ref[0, j : j + 1, :], (POOL, chans)) for j in range(tile // POOL)
        ]
        return jnp.where(valid, jnp.concatenate(pieces, axis=0), 0.0)

    t, s = t_ref[...], s_ref[...]
    d_hidden = spread(dh_ref)
    d_gate = d_hidden * s
    d_mixed = jnp.concatenate(
        [d_gate * (1.0 - t * t), d_gate * t * (1.0 - s)], axis=1
    ).astype(BF16)
    acc_ref[...] += lax.dot_general(
        joined, d_mixed, (((0,), (0,)), ((), ())), preferred_element_type=F32
    )
    d_joined = lax.dot_general(
        d_mixed, w_ref[...], (((1,), (1,)), ((), ())), preferred_element_type=F32
    )
    sig_ref[...] = (spread(dr_ref) + d_joined[:, chans:] + later_ref[...].astype(F32)).astype(BF16)
    later_ref[...] = d_joined[:, :chans].astype(BF16)

    @pl.when(i == steps - 1)
    def _():
        first_ref[...] = d_joined[:, :chans].astype(BF16)
        g_ref[...] = acc_ref[...].astype(BF16)


def add_kernel(sig_ref, extra_ref, out_ref):
    out_ref[...] = (sig_ref[...].astype(F32) + extra_ref[...].astype(F32)).astype(BF16)


def add_last(d_sig, arriving):
    samples, chans = d_sig.shape
    rows = arriving.shape[0]
    last = pl.BlockSpec((rows, chans), lambda i: (samples // rows - 1, 0))
    return pl.pallas_call(
        add_kernel,
        grid=(1,),
        out_shape=jax.ShapeDtypeStruct(d_sig.shape, BF16),
        in_specs=[last, pl.BlockSpec((rows, chans), lambda i: (0, 0))],
        out_specs=last,
        input_output_aliases={0: 0},
        name="add_last",
    )(d_sig, arriving)


def conv_forward(info, incoming, signal, w_conv):
    samples, chans = signal.shape
    tile = DILATION_STEP
    steps, pools = samples // tile, tile // POOL
    block = pl.BlockSpec((tile, chans), lambda i: (i, 0))
    sums = pl.BlockSpec((1, pools, chans), lambda i: (i, 0, 0))
    gate = jax.ShapeDtypeStruct((samples, chans), F32)
    pooled = jax.ShapeDtypeStruct((steps, pools, chans), F32)
    return pl.pallas_call(
        forward_kernel,
        grid=(steps,),
        out_shape=(gate, gate, pooled, pooled),
        in_specs=[
            pl.BlockSpec(memory_space=pltpu.SMEM),
            pl.BlockSpec((tile, chans), lambda i: (0, 0)),
            pl.BlockSpec((tile, chans), lambda i: (jnp.maximum(i - 1, 0), 0)),
            block,
            pl.BlockSpec(w_conv.shape, lambda i: (0, 0)),
        ],
        out_specs=(block, block, sums, sums),
        name="conv_forward",
    )(info, incoming, signal, signal, w_conv)


def conv_backward(info, incoming, signal, t, s, d_hidden, d_resid, w_conv):
    samples, chans = signal.shape
    tile = DILATION_STEP
    steps, pools = samples // tile, tile // POOL
    block = pl.BlockSpec((tile, chans), lambda i: (steps - 1 - i, 0))
    fixed = pl.BlockSpec((tile, chans), lambda i: (0, 0))
    sums = pl.BlockSpec((1, pools, chans), lambda i: (steps - 1 - i, 0, 0))
    whole = pl.BlockSpec(w_conv.shape, lambda i: (0, 0))
    return pl.pallas_call(
        functools.partial(backward_kernel, steps),
        grid=(steps,),
        out_shape=(
            jax.ShapeDtypeStruct((samples, chans), BF16),
            jax.ShapeDtypeStruct((tile, chans), BF16),
            jax.ShapeDtypeStruct(w_conv.shape, BF16),
        ),
        in_specs=[
            pl.BlockSpec(memory_space=pltpu.SMEM),
            fixed,
            pl.BlockSpec((tile, chans), lambda i: (jnp.maximum(steps - 2 - i, 0), 0)),
            block,
            block,
            block,
            sums,
            sums,
            whole,
        ],
        out_specs=(block, fixed, whole),
        scratch_shapes=[pltpu.VMEM(w_conv.shape, F32), pltpu.VMEM((tile, chans), BF16)],
        name="conv_backward",
    )(info, incoming, signal, signal, t, s, d_hidden, d_resid, w_conv)


def shifted(value, axis, by):
    length = lax.axis_size(axis)
    pairs = [(i, i + by) for i in range(length) if 0 <= i + by < length]
    return lax.ppermute(value, axis, pairs)


def local(signal, lengths, w_conv, w_res, w_in, w_qkv, w_out, d_out):
    stays, samples, chans = signal.shape
    width = w_in.shape[1]
    size = width // HEADS
    heads = w_out.shape[0] // size
    toks = samples // POOL
    tms, parts = lax.axis_size("tm"), lax.axis_size("stream")
    tm = lax.axis_index("tm")
    group = stays * parts
    total = toks * tms
    flat = signal.reshape(samples, chans)
    incoming = shifted(flat[samples - DILATION_STEP :], "tm", 1)
    info = jnp.stack([tm * samples, lengths[0]]).astype(jnp.int32)
    tanh_f, sig_g, h_sum, s_sum = conv_forward(info, incoming, flat, w_conv)
    h_sum = h_sum.reshape(toks, chans)
    h_part = jnp.dot(h_sum, w_res.astype(F32), precision=HIGH)
    pooled = ((s_sum.reshape(toks, chans) + h_part) / POOL).astype(BF16)[None]
    own_tok = dot("btc,cd->btd", pooled, w_in).astype(BF16)
    lens8 = jnp.broadcast_to(lengths.reshape(stays, 1, 1), (stays, 8, 128))
    g_pool, g_dout, g_len = exchange(
        "stream", 0, [("gather", pooled), ("gather", d_out), ("gather", lens8)]
    )
    group_pool = g_pool.reshape(group, toks, chans)
    group_grad = g_dout.reshape(group, toks, width)
    group_len = g_len.reshape(group, 8, 128)[:, 0, 0]
    d_ctx = dot("btd,ed->bte", group_grad, w_out).astype(BF16)
    columns = width // tms
    grad_cols = group_grad.reshape(group, toks, tms, columns).transpose(2, 0, 1, 3)
    all_pool, all_ctx, all_cols = exchange(
        "tm", 1, [("gather1", group_pool), ("gather1", d_ctx), ("scatter1", grad_cols)]
    )
    all_pool = all_pool.reshape(group, total, chans)
    all_ctx = all_ctx.reshape(group, total, heads * size)
    all_cols = all_cols.reshape(group, total, columns)
    tok = dot("btc,cd->btd", all_pool, w_in).astype(BF16).astype(F32)
    r = lax.rsqrt(jnp.mean(tok * tok, axis=-1, keepdims=True) + EPS)
    normed = (tok * r).astype(BF16)
    proj = dot("btd,de->bte", normed, w_qkv).astype(BF16)
    context, d_proj = attention(proj, all_ctx, group_len, heads, size)
    own_ctx = lax.dynamic_slice_in_dim(context, tm * toks, toks, 1)
    out_part = dot("bte,ed->btd", own_ctx, w_out).astype(BF16)
    g_out = dot("bte,btd->ed", context, all_cols)
    own_norm = lax.dynamic_slice_in_dim(normed, tm * columns, columns, 2)
    g_qkv = dot("btd,bte->de", own_norm, d_proj)
    d_normed = dot("bte,de->btd", d_proj, w_qkv)
    inner = jnp.sum(d_normed * tok, axis=-1, keepdims=True)
    d_group = (r * d_normed - tok * (r * r * r) * inner / width).astype(BF16)
    own_group = lax.dynamic_slice_in_dim(d_group, tm * toks, toks, 1)
    g_in_part = dot("btc,btd->cd", all_pool, d_group).astype(BF16)
    in_rows = chans // parts
    g_in_cols = dot("btc,btd->cd", all_pool, all_cols)
    stream = lax.axis_index("stream")
    g_in_cols = lax.dynamic_slice_in_dim(g_in_cols, stream * in_rows, in_rows, 0)
    s_out, s_group, s_in = exchange(
        "stream",
        2,
        [
            ("reduce", out_part.reshape(parts, stays, toks, width)),
            ("reduce", own_group.reshape(parts, stays, toks, width)),
            ("reduce", g_in_part.reshape(parts, in_rows, width)),
        ],
    )
    out = (own_tok.astype(F32) + s_out).astype(BF16)
    d_tok = (s_group + d_out.astype(F32)).astype(BF16)
    d_pooled = dot("btd,cd->btc", d_tok, w_in)
    d_res16 = (d_pooled / POOL).astype(BF16).reshape(toks, chans)
    g_res = lax.dot_general(h_sum, d_res16.astype(F32), (((0,), (0,)), ((), ())), precision=HIGH)
    d_hidden = lax.dot_general(
        d_res16, w_res, (((1,), (1,)), ((), ())), preferred_element_type=F32
    )
    per_tile = (samples // DILATION_STEP, DILATION_STEP // POOL, chans)
    d_sig, first, g_conv = conv_backward(
        info,
        incoming,
        flat,
        tanh_f,
        sig_g,
        d_hidden.reshape(per_tile),
        d_res16.astype(F32).reshape(per_tile),
        w_conv,
    )
    arriving = shifted(first, "tm", -1)
    d_signal = add_last(d_sig, arriving)[None]
    s_conv, s_res = exchange(
        "stream",
        3,
        [
            ("reduceb", g_conv.reshape(parts, -1, 2 * chans)),
            ("reduceb", g_res.astype(BF16).reshape(parts, -1, chans)),
        ],
    )
    t_conv, t_res = exchange(
        "tm",
        4,
        [
            ("reduceb", s_conv.reshape(tms, -1, 2 * chans)),
            ("reduceb", s_res.reshape(tms, -1, chans)),
        ],
    )
    a_conv, a_res, a_in = exchange(
        "tm",
        5,
        [
            ("gather", t_conv),
            ("gather", t_res),
            ("gather", g_in_cols.astype(BF16)),
        ],
    )
    sum_conv = a_conv.reshape(2 * chans // parts, 2 * chans).astype(F32)
    sum_res = a_res.reshape(chans // parts, chans).astype(F32)
    sum_in = s_in + a_in.transpose(1, 0, 2).reshape(in_rows, width).astype(F32)
    return (out, d_signal, sum_conv, sum_res, sum_in, g_qkv, g_out)


def solution(mesh):
    in_specs = (
        P("stream", "tm", None),
        P("stream"),
        P(),
        P(),
        P(),
        P(None, "stream"),
        P("stream", None),
        P("stream", "tm", None),
    )
    out_specs = (
        P("stream", "tm", None),
        P("stream", "tm", None),
        P("stream", None),
        P("stream", None),
        P("stream", None),
        P("tm", "stream"),
        P("stream", "tm"),
    )
    return jax.shard_map(local, mesh=mesh, in_specs=in_specs, out_specs=out_specs, check_vma=False)
```

```python
import functools
import math

import jax
import jax.numpy as jnp
from jax import lax
from jax.experimental import pallas as pl
from jax.experimental.pallas import tpu as pltpu
from jax.sharding import PartitionSpec as P

HEADS = 16
POOL = 256
DILATION_STEP = 512
EPS = 1e-05
BF16 = jnp.bfloat16
F32 = jnp.float32
HIGH = lax.Precision.HIGHEST
MESH = pl.DeviceIdType.MESH
VMEM_SPEC = pl.BlockSpec(memory_space=pltpu.VMEM)


def dot(eq, a, b):
    return jnp.einsum(eq, a, b, preferred_element_type=F32)


def exchange_kernel(axis, n, kinds, *refs):
    k = len(kinds)
    ins, outs = refs[:k], refs[k : 2 * k]
    rest = list(refs[2 * k :])
    slots = [rest.pop(0) if kind.startswith("reduce") or kind == "gatherf" else None for kind in kinds]
    send, recv, local_sem = rest
    me = lax.axis_index(axis)
    barrier = pltpu.get_barrier_semaphore()
    for d in range(1, n):
        pl.semaphore_signal(
            barrier, inc=1, device_id={axis: lax.rem(me + d, n)}, device_id_type=MESH
        )
    pl.semaphore_wait(barrier, n - 1)
    copies = []
    locals_ = []
    for j, kind in enumerate(kinds):
        for d in range(1, n):
            peer = lax.rem(me + d, n)
            src = ins[j] if kind.startswith("gather") else ins[j].at[peer]
            if kind.startswith("reduce"):
                dst = slots[j].at[d - 1]
            elif kind == "gatherf":
                dst = slots[j].at[me]
            elif kind.endswith("1"):
                dst = outs[j].at[:, me]
            else:
                dst = outs[j].at[me]
            copy = pltpu.make_async_remote_copy(
                src_ref=src,
                dst_ref=dst,
                send_sem=send.at[j, d - 1],
                recv_sem=recv.at[j, d - 1],
                device_id={axis: peer},
                device_id_type=MESH,
            )
            copy.start()
            copies.append(copy)
        if not kind.startswith("reduce"):
            src = ins[j] if kind.startswith("gather") else ins[j].at[me]
            land = slots[j] if kind == "gatherf" else outs[j]
            dst = land.at[:, me] if kind.endswith("1") else land.at[me]
            copy = pltpu.make_async_copy(src, dst, local_sem.at[j])
            copy.start()
            locals_.append(copy)
    for copy in locals_:
        copy.wait()
    for copy in copies:
        copy.wait()
    for j, kind in enumerate(kinds):
        if kind.startswith("reduce"):
            total = ins[j][me].astype(F32)
            for d in range(1, n):
                total += slots[j][d - 1].astype(F32)
            outs[j][...] = total.astype(outs[j].dtype)
        elif kind == "gatherf":
            outs[j][...] = slots[j][...].astype(F32)


def exchange(axis, collective, items):
    n = lax.axis_size(axis)
    kinds = tuple(kind for kind, _ in items)
    arrays = [array for _, array in items]
    shapes, slots = [], []
    for kind, array in items:
        inner = array.shape if kind.startswith("gather") else array.shape[1:]
        if kind.startswith("reduce"):
            shapes.append(jax.ShapeDtypeStruct(inner, BF16 if kind == "reduceb" else F32))
            slots.append(pltpu.VMEM((n - 1,) + inner, array.dtype))
        elif kind == "gatherf":
            shapes.append(jax.ShapeDtypeStruct((n,) + inner, F32))
            slots.append(pltpu.VMEM((n,) + inner, array.dtype))
        elif kind.endswith("1"):
            shapes.append(jax.ShapeDtypeStruct((inner[0], n) + inner[1:], array.dtype))
        else:
            shapes.append(jax.ShapeDtypeStruct((n,) + inner, array.dtype))
    k = len(items)
    return pl.pallas_call(
        functools.partial(exchange_kernel, axis, n, kinds),
        out_shape=shapes,
        in_specs=[VMEM_SPEC] * k,
        out_specs=[VMEM_SPEC] * k,
        scratch_shapes=slots
        + [
            pltpu.SemaphoreType.DMA((k, n - 1)),
            pltpu.SemaphoreType.DMA((k, n - 1)),
            pltpu.SemaphoreType.DMA((k,)),
        ],
        compiler_params=pltpu.CompilerParams(collective_id=collective, has_side_effects=True),
        name=f"exchange_{axis}_{collective}",
    )(*arrays)


def attention_kernel(heads, size, scale, len_ref, proj_ref, dctx_ref, ctx_ref, dproj_ref):
    stay = pl.program_id(0)
    total = proj_ref.shape[1]
    length = len_ref[stay]
    row = lax.broadcasted_iota(jnp.int32, (total, total), 0)
    col = lax.broadcasted_iota(jnp.int32, (total, total), 1)
    allowed = (col <= row) & (col * POOL < length)
    nt = (((1,), (1,)), ((), ()))
    tn = (((0,), (0,)), ((), ()))
    for h in range(heads):
        base = h * 3 * size
        query = proj_ref[0, :, base : base + size]
        key = proj_ref[0, :, base + size : base + 2 * size]
        value = proj_ref[0, :, base + 2 * size : base + 3 * size]
        dctx = dctx_ref[0, :, h * size : (h + 1) * size]
        scores = lax.dot_general(query, key, nt, preferred_element_type=F32) * scale
        scores = jnp.where(allowed, scores, -1e30)
        top = jnp.max(scores, axis=-1, keepdims=True)
        weights = jnp.exp(scores - top)
        prob = weights / jnp.sum(weights, axis=-1, keepdims=True)
        prob16 = prob.astype(BF16)
        context = jnp.dot(prob16, value, preferred_element_type=F32)
        ctx_ref[0, :, h * size : (h + 1) * size] = context.astype(BF16)
        d_prob = lax.dot_general(dctx, value, nt, preferred_element_type=F32)
        d_score = prob * (d_prob - jnp.sum(d_prob * prob, axis=-1, keepdims=True))
        d16 = d_score.astype(BF16)
        d_query = scale * jnp.dot(d16, key, preferred_element_type=F32)
        d_key = scale * lax.dot_general(d16, query, tn, preferred_element_type=F32)
        d_value = lax.dot_general(prob16, dctx, tn, preferred_element_type=F32)
        dproj_ref[0, :, base : base + size] = d_query.astype(BF16)
        dproj_ref[0, :, base + size : base + 2 * size] = d_key.astype(BF16)
        dproj_ref[0, :, base + 2 * size : base + 3 * size] = d_value.astype(BF16)


def attention(proj, d_context, group_len, heads, size):
    group, total, width = proj.shape
    inner = heads * size
    wide = pl.BlockSpec((1, total, width), lambda s: (s, 0, 0))
    thin = pl.BlockSpec((1, total, inner), lambda s: (s, 0, 0))
    return pl.pallas_call(
        functools.partial(attention_kernel, heads, size, 1.0 / math.sqrt(size)),
        grid=(group,),
        out_shape=(
            jax.ShapeDtypeStruct((group, total, inner), BF16),
            jax.ShapeDtypeStruct((group, total, width), BF16),
        ),
        in_specs=[pl.BlockSpec(memory_space=pltpu.SMEM), wide, thin],
        out_specs=(thin, wide),
        name="attention",
    )(group_len, proj, d_context)


def riding_copies(axis, kinds, ins, slots, send, recv, keep):
    n = lax.axis_size(axis)
    me = lax.axis_index(axis)
    copies = []
    for j, kind in enumerate(kinds):
        for d in range(1, n):
            peer = lax.rem(me + d, n)
            copies.append(
                pltpu.make_async_remote_copy(
                    src_ref=ins[j] if kind == "gather1" else ins[j].at[peer],
                    dst_ref=slots[j].at[d - 1] if kind == "reduce" else slots[j].at[:, me],
                    send_sem=send.at[j, d - 1],
                    recv_sem=recv.at[j, d - 1],
                    device_id={axis: peer},
                    device_id_type=MESH,
                )
            )
        if kind != "reduce":
            src = ins[j] if kind == "gather1" else ins[j].at[me]
            copies.append(pltpu.make_async_copy(src, slots[j].at[:, me], keep.at[j]))
    return copies


def ride_start(axis, kinds, ins, slots, send, recv, keep):
    n = lax.axis_size(axis)
    me = lax.axis_index(axis)
    barrier = pltpu.get_barrier_semaphore()
    for d in range(1, n):
        pl.semaphore_signal(
            barrier, inc=1, device_id={axis: lax.rem(me + d, n)}, device_id_type=MESH
        )
    pl.semaphore_wait(barrier, n - 1)
    for copy in riding_copies(axis, kinds, ins, slots, send, recv, keep):
        copy.start()


def ride_finish(axis, kinds, ins, outs, slots, send, recv, keep):
    n = lax.axis_size(axis)
    me = lax.axis_index(axis)
    for copy in riding_copies(axis, kinds, ins, slots, send, recv, keep):
        copy.wait()
    for j, kind in enumerate(kinds):
        if kind == "reduce":
            sum_ = ins[j][me].astype(F32)
            for d in range(1, n):
                sum_ += slots[j][d - 1].astype(F32)
            outs[j][...] = sum_
        else:
            outs[j][...] = slots[j][...]


def ride_shapes(n, items):
    shapes, scratch = [], []
    for kind, array in items:
        inner = array.shape if kind == "gather1" else array.shape[1:]
        if kind == "reduce":
            shapes.append(jax.ShapeDtypeStruct(inner, F32))
            scratch.append(pltpu.VMEM((n - 1,) + inner, array.dtype))
        else:
            out = (inner[0], n) + inner[1:]
            shapes.append(jax.ShapeDtypeStruct(out, array.dtype))
            scratch.append(pltpu.VMEM(out, array.dtype))
    k = len(items)
    sems = [pltpu.SemaphoreType.DMA((k, n - 1))] * 2 + [pltpu.SemaphoreType.DMA((k,))]
    specs = [pl.BlockSpec(a.shape, functools.partial(origin, a.ndim)) for _, a in items]
    outs = [pl.BlockSpec(a.shape, functools.partial(origin, len(a.shape))) for a in shapes]
    return shapes, scratch + sems, specs, outs


def origin(rank, i):
    return (0,) * rank


def tile_valid(info_ref, tile, step):
    row = lax.broadcasted_iota(jnp.int32, (tile, 1), 0)
    return info_ref[0] + step * tile + row < info_ref[1]


def joined_tile(first, in_ref, past_ref, cur_ref):
    past = jnp.where(first, in_ref[...], past_ref[...])
    return jnp.concatenate([past, cur_ref[...]], axis=1)


def forward_kernel(
    steps, axis, kinds, info_ref, in_ref, past_ref, cur_ref, w_ref, *refs
):
    k = len(kinds)
    ins, (t_ref, s_ref, hs_ref, ss_ref) = refs[:k], refs[k : k + 4]
    outs, slots, sems = refs[k + 4 : 2 * k + 4], refs[2 * k + 4 : 3 * k + 4], refs[3 * k + 4 :]
    i = pl.program_id(0)

    @pl.when(i == 0)
    def _():
        ride_start(axis, kinds, ins, slots, *sems)

    tile, chans = cur_ref.shape
    joined = joined_tile(i == 0, in_ref, past_ref, cur_ref)
    mixed = jnp.dot(joined, w_ref[...], preferred_element_type=F32)
    t = jnp.tanh(mixed[:, :chans])
    s = jax.nn.sigmoid(mixed[:, chans:])
    t_ref[...] = t
    s_ref[...] = s
    valid = tile_valid(info_ref, tile, i)
    hidden = jnp.where(valid, (t * s).astype(BF16).astype(F32), 0.0)
    kept = jnp.where(valid, cur_ref[...].astype(F32), 0.0)
    for j in range(tile // POOL):
        rows = slice(j * POOL, (j + 1) * POOL)
        hs_ref[0, j : j + 1, :] = jnp.sum(hidden[rows], axis=0, keepdims=True)
        ss_ref[0, j : j + 1, :] = jnp.sum(kept[rows], axis=0, keepdims=True)

    @pl.when(i == steps - 1)
    def _():
        ride_finish(axis, kinds, ins, outs, slots, *sems)


def backward_kernel(
    steps, axis, kinds, info_ref, in_ref, past_ref, cur_ref, t_ref, s_ref, dh_ref, dr_ref, w_ref,
    *refs,
):
    k = len(kinds)
    ins, (sig_ref, first_ref, g_ref) = refs[:k], refs[k : k + 3]
    outs, (acc_ref, later_ref) = refs[k + 3 : 2 * k + 3], refs[2 * k + 3 : 2 * k + 5]
    slots, sems = refs[2 * k + 5 : 3 * k + 5], refs[3 * k + 5 :]
    i = pl.program_id(0)

    @pl.when(i == 0)
    def _():
        ride_start(axis, kinds, ins, slots, *sems)

    step = steps - 1 - i
    tile, chans = cur_ref.shape

    @pl.when(i == 0)
    def _():
        acc_ref[...] = jnp.zeros_like(acc_ref)
        later_ref[...] = jnp.zeros_like(later_ref)

    joined = joined_tile(step == 0, in_ref, past_ref, cur_ref)
    valid = tile_valid(info_ref, tile, step)

    def spread(ref):
        pieces = [
            jnp.broadcast_to(ref[0, j : j + 1, :], (POOL, chans)) for j in range(tile // POOL)
        ]
        return jnp.where(valid, jnp.concatenate(pieces, axis=0), 0.0)

    t, s = t_ref[...], s_ref[...]
    d_hidden = spread(dh_ref)
    d_gate = d_hidden * s
    d_mixed = jnp.concatenate(
        [d_gate * (1.0 - t * t), d_gate * t * (1.0 - s)], axis=1
    ).astype(BF16)
    acc_ref[...] += lax.dot_general(
        joined, d_mixed, (((0,), (0,)), ((), ())), preferred_element_type=F32
    )
    d_joined = lax.dot_general(
        d_mixed, w_ref[...], (((1,), (1,)), ((), ())), preferred_element_type=F32
    )
    sig_ref[...] = (spread(dr_ref) + d_joined[:, chans:] + later_ref[...].astype(F32)).astype(BF16)
    later_ref[...] = d_joined[:, :chans].astype(BF16)

    @pl.when(i == steps - 1)
    def _():
        first_ref[...] = d_joined[:, :chans].astype(BF16)
        g_ref[...] = acc_ref[...].astype(BF16)
        ride_finish(axis, kinds, ins, outs, slots, *sems)


def add_kernel(sig_ref, extra_ref, out_ref):
    out_ref[...] = (sig_ref[...].astype(F32) + extra_ref[...].astype(F32)).astype(BF16)


def add_last(d_sig, arriving):
    samples, chans = d_sig.shape
    rows = arriving.shape[0]
    last = pl.BlockSpec((rows, chans), lambda i: (samples // rows - 1, 0))
    return pl.pallas_call(
        add_kernel,
        grid=(1,),
        out_shape=jax.ShapeDtypeStruct(d_sig.shape, BF16),
        in_specs=[last, pl.BlockSpec((rows, chans), lambda i: (0, 0))],
        out_specs=last,
        input_output_aliases={0: 0},
        name="add_last",
    )(d_sig, arriving)


def conv_forward(info, incoming, signal, w_conv, axis, collective, items):
    kinds = tuple(kind for kind, _ in items)
    shapes, scratch, specs, out_specs = ride_shapes(lax.axis_size(axis), items)
    samples, chans = signal.shape
    tile = DILATION_STEP
    steps, pools = samples // tile, tile // POOL
    block = pl.BlockSpec((tile, chans), lambda i: (i, 0))
    sums = pl.BlockSpec((1, pools, chans), lambda i: (i, 0, 0))
    gate = jax.ShapeDtypeStruct((samples, chans), F32)
    pooled = jax.ShapeDtypeStruct((steps, pools, chans), F32)
    return pl.pallas_call(
        functools.partial(forward_kernel, steps, axis, kinds),
        grid=(steps,),
        out_shape=[gate, gate, pooled, pooled] + shapes,
        in_specs=[
            pl.BlockSpec(memory_space=pltpu.SMEM),
            pl.BlockSpec((tile, chans), lambda i: (0, 0)),
            pl.BlockSpec((tile, chans), lambda i: (jnp.maximum(i - 1, 0), 0)),
            block,
            pl.BlockSpec(w_conv.shape, lambda i: (0, 0)),
        ]
        + specs,
        out_specs=[block, block, sums, sums] + out_specs,
        scratch_shapes=scratch,
        compiler_params=pltpu.CompilerParams(collective_id=collective, has_side_effects=True),
        name="conv_forward",
    )(info, incoming, signal, signal, w_conv, *[array for _, array in items])


def conv_backward(
    info, incoming, signal, t, s, d_hidden, d_resid, w_conv, axis, collective, items
):
    kinds = tuple(kind for kind, _ in items)
    shapes, scratch, specs, out_specs = ride_shapes(lax.axis_size(axis), items)
    samples, chans = signal.shape
    tile = DILATION_STEP
    steps, pools = samples // tile, tile // POOL
    block = pl.BlockSpec((tile, chans), lambda i: (steps - 1 - i, 0))
    fixed = pl.BlockSpec((tile, chans), lambda i: (0, 0))
    sums = pl.BlockSpec((1, pools, chans), lambda i: (steps - 1 - i, 0, 0))
    whole = pl.BlockSpec(w_conv.shape, lambda i: (0, 0))
    return pl.pallas_call(
        functools.partial(backward_kernel, steps, axis, kinds),
        grid=(steps,),
        out_shape=[
            jax.ShapeDtypeStruct((samples, chans), BF16),
            jax.ShapeDtypeStruct((tile, chans), BF16),
            jax.ShapeDtypeStruct(w_conv.shape, BF16),
        ]
        + shapes,
        in_specs=[
            pl.BlockSpec(memory_space=pltpu.SMEM),
            fixed,
            pl.BlockSpec((tile, chans), lambda i: (jnp.maximum(steps - 2 - i, 0), 0)),
            block,
            block,
            block,
            sums,
            sums,
            whole,
        ]
        + specs,
        out_specs=[block, fixed, whole] + out_specs,
        scratch_shapes=[pltpu.VMEM(w_conv.shape, F32), pltpu.VMEM((tile, chans), BF16)] + scratch,
        compiler_params=pltpu.CompilerParams(collective_id=collective, has_side_effects=True),
        name="conv_backward",
    )(info, incoming, signal, signal, t, s, d_hidden, d_resid, w_conv, *[a for _, a in items])


def shifted(value, axis, by):
    length = lax.axis_size(axis)
    pairs = [(i, i + by) for i in range(length) if 0 <= i + by < length]
    return lax.ppermute(value, axis, pairs)


def local(signal, lengths, w_conv, w_res, w_in, w_qkv, w_out, d_out):
    stays, samples, chans = signal.shape
    width = w_in.shape[1]
    size = width // HEADS
    heads = w_out.shape[0] // size
    toks = samples // POOL
    tms, parts = lax.axis_size("tm"), lax.axis_size("stream")
    tm = lax.axis_index("tm")
    group = stays * parts
    total = toks * tms
    flat = signal.reshape(samples, chans)
    incoming = shifted(flat[samples - DILATION_STEP :], "tm", 1)
    info = jnp.stack([tm * samples, lengths[0]]).astype(jnp.int32)
    lens8 = jnp.broadcast_to(lengths.reshape(stays, 1, 1), (stays, 8, 128))
    g_dout, g_len = exchange("stream", 0, [("gather", d_out), ("gather", lens8)])
    group_grad = g_dout.reshape(group, toks, width)
    group_len = g_len.reshape(group, 8, 128)[:, 0, 0]
    d_ctx = dot("btd,ed->bte", group_grad, w_out).astype(BF16)
    columns = width // tms
    grad_cols = group_grad.reshape(group, toks, tms, columns).transpose(2, 0, 1, 3)
    tanh_f, sig_g, h_sum, s_sum, all_ctx, all_cols = conv_forward(
        info, incoming, flat, w_conv, "tm", 6, [("gather1", d_ctx), ("scatter1", grad_cols)]
    )
    h_sum = h_sum.reshape(toks, chans)
    h_part = jnp.dot(h_sum, w_res.astype(F32), precision=HIGH)
    pooled = ((s_sum.reshape(toks, chans) + h_part) / POOL).astype(BF16)[None]
    own_tok = dot("btc,cd->btd", pooled, w_in).astype(BF16)
    (stay_pool,) = exchange("tm", 1, [("gather1", pooled)])
    (all_pool,) = exchange("stream", 7, [("gather", stay_pool.reshape(stays, total, chans))])
    all_pool = all_pool.reshape(group, total, chans)
    all_ctx = all_ctx.reshape(group, total, heads * size)
    all_cols = all_cols.reshape(group, total, columns)
    tok = dot("btc,cd->btd", all_pool, w_in).astype(BF16).astype(F32)
    r = lax.rsqrt(jnp.mean(tok * tok, axis=-1, keepdims=True) + EPS)
    normed = (tok * r).astype(BF16)
    proj = dot("btd,de->bte", normed, w_qkv).astype(BF16)
    context, d_proj = attention(proj, all_ctx, group_len, heads, size)
    own_ctx = lax.dynamic_slice_in_dim(context, tm * toks, toks, 1)
    out_part = dot("bte,ed->btd", own_ctx, w_out).astype(BF16)
    g_out = dot("bte,btd->ed", context, all_cols)
    own_norm = lax.dynamic_slice_in_dim(normed, tm * columns, columns, 2)
    g_qkv = dot("btd,bte->de", own_norm, d_proj)
    d_normed = dot("bte,de->btd", d_proj, w_qkv)
    inner = jnp.sum(d_normed * tok, axis=-1, keepdims=True)
    d_group = (r * d_normed - tok * (r * r * r) * inner / width).astype(BF16)
    own_group = lax.dynamic_slice_in_dim(d_group, tm * toks, toks, 1)
    g_in_part = dot("btc,btd->cd", all_pool, d_group).astype(BF16)
    in_rows = chans // parts
    g_in_cols = dot("btc,btd->cd", all_pool, all_cols)
    stream = lax.axis_index("stream")
    g_in_cols = lax.dynamic_slice_in_dim(g_in_cols, stream * in_rows, in_rows, 0)
    (s_group,) = exchange(
        "stream", 2, [("reduce", own_group.reshape(parts, stays, toks, width))]
    )
    d_tok = (s_group + d_out.astype(F32)).astype(BF16)
    d_pooled = dot("btd,cd->btc", d_tok, w_in)
    d_res16 = (d_pooled / POOL).astype(BF16).reshape(toks, chans)
    g_res = lax.dot_general(h_sum, d_res16.astype(F32), (((0,), (0,)), ((), ())), precision=HIGH)
    d_hidden = lax.dot_general(
        d_res16, w_res, (((1,), (1,)), ((), ())), preferred_element_type=F32
    )
    per_tile = (samples // DILATION_STEP, DILATION_STEP // POOL, chans)
    d_sig, first, g_conv, s_out, s_in = conv_backward(
        info,
        incoming,
        flat,
        tanh_f,
        sig_g,
        d_hidden.reshape(per_tile),
        d_res16.astype(F32).reshape(per_tile),
        w_conv,
        "stream",
        8,
        [
            ("reduce", out_part.reshape(parts, stays, toks, width)),
            ("reduce", g_in_part.reshape(parts, in_rows, width)),
        ],
    )
    out = (own_tok.astype(F32) + s_out).astype(BF16)
    arriving = shifted(first, "tm", -1)
    d_signal = add_last(d_sig, arriving)[None]
    s_conv, s_res = exchange(
        "stream",
        3,
        [
            ("reduceb", g_conv.reshape(parts, -1, 2 * chans)),
            ("reduceb", g_res.astype(BF16).reshape(parts, -1, chans)),
        ],
    )
    t_conv, t_res = exchange(
        "tm",
        4,
        [
            ("reduceb", s_conv.reshape(tms, -1, 2 * chans)),
            ("reduceb", s_res.reshape(tms, -1, chans)),
        ],
    )
    a_conv, a_res, a_in = exchange(
        "tm",
        5,
        [
            ("gatherf", t_conv),
            ("gatherf", t_res),
            ("gatherf", g_in_cols.astype(BF16)),
        ],
    )
    sum_conv = a_conv.reshape(2 * chans // parts, 2 * chans).astype(F32)
    sum_res = a_res.reshape(chans // parts, chans).astype(F32)
    sum_in = s_in + a_in.transpose(1, 0, 2).reshape(in_rows, width).astype(F32)
    return (out, d_signal, sum_conv, sum_res, sum_in, g_qkv, g_out)


def solution(mesh):
    in_specs = (
        P("stream", "tm", None),
        P("stream"),
        P(),
        P(),
        P(),
        P(None, "stream"),
        P("stream", None),
        P("stream", "tm", None),
    )
    out_specs = (
        P("stream", "tm", None),
        P("stream", "tm", None),
        P("stream", None),
        P("stream", None),
        P("stream", None),
        P("tm", "stream"),
        P("stream", "tm"),
    )
    return jax.shard_map(local, mesh=mesh, in_specs=in_specs, out_specs=out_specs, check_vma=False)
```

```python
import functools
import math

import jax
import jax.numpy as jnp
from jax import lax
from jax.experimental import pallas as pl
from jax.experimental.pallas import tpu as pltpu
from jax.sharding import PartitionSpec as P

HEADS = 16
POOL = 256
DILATION_STEP = 512
EPS = 1e-05
BF16 = jnp.bfloat16
F32 = jnp.float32
HIGH = lax.Precision.HIGHEST
MESH = pl.DeviceIdType.MESH
VMEM_SPEC = pl.BlockSpec(memory_space=pltpu.VMEM)


def dot(eq, a, b):
    return jnp.einsum(eq, a, b, preferred_element_type=F32)


def exchange_kernel(axis, n, kinds, *refs):
    k = len(kinds)
    ins, outs = refs[:k], refs[k : 2 * k]
    rest = list(refs[2 * k :])
    slots = [rest.pop(0) if kind.startswith("reduce") or kind == "gatherf" else None for kind in kinds]
    send, recv, local_sem = rest
    me = lax.axis_index(axis)
    barrier = pltpu.get_barrier_semaphore()
    for d in range(1, n):
        pl.semaphore_signal(
            barrier, inc=1, device_id={axis: lax.rem(me + d, n)}, device_id_type=MESH
        )
    pl.semaphore_wait(barrier, n - 1)
    copies = []
    locals_ = []
    for j, kind in enumerate(kinds):
        for d in range(1, n):
            peer = lax.rem(me + d, n)
            src = ins[j] if kind.startswith("gather") else ins[j].at[peer]
            if kind.startswith("reduce"):
                dst = slots[j].at[d - 1]
            elif kind == "gatherf":
                dst = slots[j].at[me]
            elif kind.endswith("1"):
                dst = outs[j].at[:, me]
            else:
                dst = outs[j].at[me]
            copy = pltpu.make_async_remote_copy(
                src_ref=src,
                dst_ref=dst,
                send_sem=send.at[j, d - 1],
                recv_sem=recv.at[j, d - 1],
                device_id={axis: peer},
                device_id_type=MESH,
            )
            copy.start()
            copies.append(copy)
        if not kind.startswith("reduce"):
            src = ins[j] if kind.startswith("gather") else ins[j].at[me]
            land = slots[j] if kind == "gatherf" else outs[j]
            dst = land.at[:, me] if kind.endswith("1") else land.at[me]
            copy = pltpu.make_async_copy(src, dst, local_sem.at[j])
            copy.start()
            locals_.append(copy)
    for copy in locals_:
        copy.wait()
    for copy in copies:
        copy.wait()
    for j, kind in enumerate(kinds):
        if kind.startswith("reduce"):
            total = ins[j][me].astype(F32)
            for d in range(1, n):
                total += slots[j][d - 1].astype(F32)
            outs[j][...] = total.astype(outs[j].dtype)
        elif kind == "gatherf":
            outs[j][...] = slots[j][...].astype(F32)


def exchange(axis, collective, items):
    n = lax.axis_size(axis)
    kinds = tuple(kind for kind, _ in items)
    arrays = [array for _, array in items]
    shapes, slots = [], []
    for kind, array in items:
        inner = array.shape if kind.startswith("gather") else array.shape[1:]
        if kind.startswith("reduce"):
            shapes.append(jax.ShapeDtypeStruct(inner, BF16 if kind == "reduceb" else F32))
            slots.append(pltpu.VMEM((n - 1,) + inner, array.dtype))
        elif kind == "gatherf":
            shapes.append(jax.ShapeDtypeStruct((n,) + inner, F32))
            slots.append(pltpu.VMEM((n,) + inner, array.dtype))
        elif kind.endswith("1"):
            shapes.append(jax.ShapeDtypeStruct((inner[0], n) + inner[1:], array.dtype))
        else:
            shapes.append(jax.ShapeDtypeStruct((n,) + inner, array.dtype))
    k = len(items)
    return pl.pallas_call(
        functools.partial(exchange_kernel, axis, n, kinds),
        out_shape=shapes,
        in_specs=[VMEM_SPEC] * k,
        out_specs=[VMEM_SPEC] * k,
        scratch_shapes=slots
        + [
            pltpu.SemaphoreType.DMA((k, n - 1)),
            pltpu.SemaphoreType.DMA((k, n - 1)),
            pltpu.SemaphoreType.DMA((k,)),
        ],
        compiler_params=pltpu.CompilerParams(collective_id=collective, has_side_effects=True),
        name=f"exchange_{axis}_{collective}",
    )(*arrays)


def attention_kernel(heads, size, scale, len_ref, proj_ref, dctx_ref, ctx_ref, dproj_ref):
    stay = pl.program_id(0)
    total = proj_ref.shape[1]
    length = len_ref[stay]
    row = lax.broadcasted_iota(jnp.int32, (total, total), 0)
    col = lax.broadcasted_iota(jnp.int32, (total, total), 1)
    allowed = (col <= row) & (col * POOL < length)
    nt = (((1,), (1,)), ((), ()))
    tn = (((0,), (0,)), ((), ()))
    for h in range(heads):
        base = h * 3 * size
        query = proj_ref[0, :, base : base + size]
        key = proj_ref[0, :, base + size : base + 2 * size]
        value = proj_ref[0, :, base + 2 * size : base + 3 * size]
        dctx = dctx_ref[0, :, h * size : (h + 1) * size]
        scores = lax.dot_general(query, key, nt, preferred_element_type=F32) * scale
        scores = jnp.where(allowed, scores, -1e30)
        top = jnp.max(scores, axis=-1, keepdims=True)
        weights = jnp.exp(scores - top)
        prob = weights / jnp.sum(weights, axis=-1, keepdims=True)
        prob16 = prob.astype(BF16)
        context = jnp.dot(prob16, value, preferred_element_type=F32)
        ctx_ref[0, :, h * size : (h + 1) * size] = context.astype(BF16)
        d_prob = lax.dot_general(dctx, value, nt, preferred_element_type=F32)
        d_score = prob * (d_prob - jnp.sum(d_prob * prob, axis=-1, keepdims=True))
        d16 = d_score.astype(BF16)
        d_query = scale * jnp.dot(d16, key, preferred_element_type=F32)
        d_key = scale * lax.dot_general(d16, query, tn, preferred_element_type=F32)
        d_value = lax.dot_general(prob16, dctx, tn, preferred_element_type=F32)
        dproj_ref[0, :, base : base + size] = d_query.astype(BF16)
        dproj_ref[0, :, base + size : base + 2 * size] = d_key.astype(BF16)
        dproj_ref[0, :, base + 2 * size : base + 3 * size] = d_value.astype(BF16)


def attention(proj, d_context, group_len, heads, size):
    group, total, width = proj.shape
    inner = heads * size
    wide = pl.BlockSpec((1, total, width), lambda s: (s, 0, 0))
    thin = pl.BlockSpec((1, total, inner), lambda s: (s, 0, 0))
    return pl.pallas_call(
        functools.partial(attention_kernel, heads, size, 1.0 / math.sqrt(size)),
        grid=(group,),
        out_shape=(
            jax.ShapeDtypeStruct((group, total, inner), BF16),
            jax.ShapeDtypeStruct((group, total, width), BF16),
        ),
        in_specs=[pl.BlockSpec(memory_space=pltpu.SMEM), wide, thin],
        out_specs=(thin, wide),
        name="attention",
    )(group_len, proj, d_context)


def riding_copies(axis, kinds, ins, slots, send, recv, keep):
    n = lax.axis_size(axis)
    me = lax.axis_index(axis)
    copies = []
    for j, kind in enumerate(kinds):
        for d in range(1, n):
            peer = lax.rem(me + d, n)
            copies.append(
                pltpu.make_async_remote_copy(
                    src_ref=ins[j] if kind == "gather1" else ins[j].at[peer],
                    dst_ref=slots[j].at[d - 1] if kind == "reduce" else slots[j].at[:, me],
                    send_sem=send.at[j, d - 1],
                    recv_sem=recv.at[j, d - 1],
                    device_id={axis: peer},
                    device_id_type=MESH,
                )
            )
        if kind != "reduce":
            src = ins[j] if kind == "gather1" else ins[j].at[me]
            copies.append(pltpu.make_async_copy(src, slots[j].at[:, me], keep.at[j]))
    return copies


def ride_start(axis, kinds, ins, slots, send, recv, keep):
    n = lax.axis_size(axis)
    me = lax.axis_index(axis)
    barrier = pltpu.get_barrier_semaphore()
    for d in range(1, n):
        pl.semaphore_signal(
            barrier, inc=1, device_id={axis: lax.rem(me + d, n)}, device_id_type=MESH
        )
    pl.semaphore_wait(barrier, n - 1)
    for copy in riding_copies(axis, kinds, ins, slots, send, recv, keep):
        copy.start()


def ride_finish(axis, kinds, ins, outs, slots, send, recv, keep):
    n = lax.axis_size(axis)
    me = lax.axis_index(axis)
    for copy in riding_copies(axis, kinds, ins, slots, send, recv, keep):
        copy.wait()
    for j, kind in enumerate(kinds):
        if kind == "reduce":
            sum_ = ins[j][me].astype(F32)
            for d in range(1, n):
                sum_ += slots[j][d - 1].astype(F32)
            outs[j][...] = sum_
        else:
            outs[j][...] = slots[j][...]


def ride_shapes(n, items):
    shapes, scratch = [], []
    for kind, array in items:
        inner = array.shape if kind == "gather1" else array.shape[1:]
        if kind == "reduce":
            shapes.append(jax.ShapeDtypeStruct(inner, F32))
            scratch.append(pltpu.VMEM((n - 1,) + inner, array.dtype))
        else:
            out = (inner[0], n) + inner[1:]
            shapes.append(jax.ShapeDtypeStruct(out, array.dtype))
            scratch.append(pltpu.VMEM(out, array.dtype))
    k = len(items)
    sems = [pltpu.SemaphoreType.DMA((k, n - 1))] * 2 + [pltpu.SemaphoreType.DMA((k,))]
    specs = [pl.BlockSpec(a.shape, functools.partial(origin, a.ndim)) for _, a in items]
    outs = [pl.BlockSpec(a.shape, functools.partial(origin, len(a.shape))) for a in shapes]
    return shapes, scratch + sems, specs, outs


def origin(rank, i):
    return (0,) * rank


def tile_valid(info_ref, tile, step):
    row = lax.broadcasted_iota(jnp.int32, (tile, 1), 0)
    return info_ref[0] + step * tile + row < info_ref[1]


def joined_tile(first, in_ref, past_ref, cur_ref):
    past = jnp.where(first, in_ref[...], past_ref[...])
    return jnp.concatenate([past, cur_ref[...]], axis=1)


def forward_kernel(
    steps, axis, kinds, info_ref, in_ref, past_ref, cur_ref, w_ref, *refs
):
    k = len(kinds)
    ins, (t_ref, s_ref, hs_ref, ss_ref) = refs[:k], refs[k : k + 4]
    outs, slots, sems = refs[k + 4 : 2 * k + 4], refs[2 * k + 4 : 3 * k + 4], refs[3 * k + 4 :]
    i = pl.program_id(0)

    @pl.when(i == 0)
    def _():
        ride_start(axis, kinds, ins, slots, *sems)

    tile, chans = cur_ref.shape
    joined = joined_tile(i == 0, in_ref, past_ref, cur_ref)
    mixed = jnp.dot(joined, w_ref[...], preferred_element_type=F32)
    t = jnp.tanh(mixed[:, :chans])
    s = jax.nn.sigmoid(mixed[:, chans:])
    t_ref[...] = t
    s_ref[...] = s
    valid = tile_valid(info_ref, tile, i)
    hidden = jnp.where(valid, (t * s).astype(BF16).astype(F32), 0.0)
    kept = jnp.where(valid, cur_ref[...].astype(F32), 0.0)
    for j in range(tile // POOL):
        rows = slice(j * POOL, (j + 1) * POOL)
        hs_ref[0, j : j + 1, :] = jnp.sum(hidden[rows], axis=0, keepdims=True)
        ss_ref[0, j : j + 1, :] = jnp.sum(kept[rows], axis=0, keepdims=True)

    @pl.when(i == steps - 1)
    def _():
        ride_finish(axis, kinds, ins, outs, slots, *sems)


def backward_kernel(
    steps, axis, kinds, info_ref, in_ref, past_ref, cur_ref, t_ref, s_ref, dh_ref, dr_ref, w_ref,
    *refs,
):
    k = len(kinds)
    ins, (sig_ref, first_ref, g_ref) = refs[:k], refs[k : k + 3]
    outs, (acc_ref, later_ref) = refs[k + 3 : 2 * k + 3], refs[2 * k + 3 : 2 * k + 5]
    slots, sems = refs[2 * k + 5 : 3 * k + 5], refs[3 * k + 5 :]
    i = pl.program_id(0)

    @pl.when(i == 0)
    def _():
        ride_start(axis, kinds, ins, slots, *sems)

    step = steps - 1 - i
    tile, chans = cur_ref.shape

    @pl.when(i == 0)
    def _():
        acc_ref[...] = jnp.zeros_like(acc_ref)
        later_ref[...] = jnp.zeros_like(later_ref)

    joined = joined_tile(step == 0, in_ref, past_ref, cur_ref)
    valid = tile_valid(info_ref, tile, step)

    def spread(ref):
        pieces = [
            jnp.broadcast_to(ref[0, j : j + 1, :], (POOL, chans)) for j in range(tile // POOL)
        ]
        return jnp.where(valid, jnp.concatenate(pieces, axis=0), 0.0)

    t, s = t_ref[...], s_ref[...]
    d_hidden = spread(dh_ref)
    d_gate = d_hidden * s
    d_mixed = jnp.concatenate(
        [d_gate * (1.0 - t * t), d_gate * t * (1.0 - s)], axis=1
    ).astype(BF16)
    acc_ref[...] += lax.dot_general(
        joined, d_mixed, (((0,), (0,)), ((), ())), preferred_element_type=F32
    )
    d_joined = lax.dot_general(
        d_mixed, w_ref[...], (((1,), (1,)), ((), ())), preferred_element_type=F32
    )
    sig_ref[...] = (spread(dr_ref) + d_joined[:, chans:] + later_ref[...].astype(F32)).astype(BF16)
    later_ref[...] = d_joined[:, :chans].astype(BF16)

    @pl.when(i == steps - 1)
    def _():
        first_ref[...] = d_joined[:, :chans].astype(BF16)
        g_ref[...] = acc_ref[...].astype(BF16)
        ride_finish(axis, kinds, ins, outs, slots, *sems)


def final_kernel(axis, n, *refs):
    ins, outs, slots, mine, lands = refs[:3], refs[3:6], refs[6:8], refs[8:10], refs[10:13]
    send, recv, keep = refs[13:]
    me = lax.axis_index(axis)
    barrier = pltpu.get_barrier_semaphore()
    for d in range(1, n):
        pl.semaphore_signal(
            barrier, inc=1, device_id={axis: lax.rem(me + d, n)}, device_id_type=MESH
        )
    pl.semaphore_wait(barrier, n - 1)

    def push(row, d, src, dst):
        copy = pltpu.make_async_remote_copy(
            src_ref=src,
            dst_ref=dst,
            send_sem=send.at[row, d - 1],
            recv_sem=recv.at[row, d - 1],
            device_id={axis: lax.rem(me + d, n)},
            device_id_type=MESH,
        )
        copy.start()
        return copy

    parts = [
        push(j, d, ins[j].at[lax.rem(me + d, n)], slots[j].at[d - 1])
        for j in range(2)
        for d in range(1, n)
    ]
    rest = [push(2, d, ins[2], lands[2].at[me]) for d in range(1, n)]
    for copy in parts:
        copy.wait()
    for j in range(2):
        total = ins[j][me].astype(F32)
        for d in range(1, n):
            total += slots[j][d - 1].astype(F32)
        mine[j][...] = total.astype(BF16)
    for j, src in enumerate((mine[0], mine[1], ins[2])):
        copy = pltpu.make_async_copy(src, lands[j].at[me], keep.at[j])
        copy.start()
        rest.append(copy)
    rest += [push(3 + j, d, mine[j], lands[j].at[me]) for j in range(2) for d in range(1, n)]
    for copy in rest:
        copy.wait()
    for j in range(3):
        outs[j][...] = lands[j][...].astype(F32)


def final_sums(axis, collective, conv, res, cols):
    n = lax.axis_size(axis)
    shapes = [conv.shape, res.shape, (n,) + cols.shape]
    sums = [conv.shape[1:], res.shape[1:]]
    return pl.pallas_call(
        functools.partial(final_kernel, axis, n),
        out_shape=[jax.ShapeDtypeStruct(a, F32) for a in shapes],
        in_specs=[VMEM_SPEC] * 3,
        out_specs=[VMEM_SPEC] * 3,
        scratch_shapes=[pltpu.VMEM((n - 1,) + a, BF16) for a in sums]
        + [pltpu.VMEM(a, BF16) for a in sums]
        + [pltpu.VMEM(a, BF16) for a in shapes]
        + [pltpu.SemaphoreType.DMA((5, n - 1))] * 2
        + [pltpu.SemaphoreType.DMA((3,))],
        compiler_params=pltpu.CompilerParams(collective_id=collective, has_side_effects=True),
        name="final_sums",
    )(conv, res, cols)


def conv_forward(info, incoming, signal, w_conv, axis, collective, items):
    kinds = tuple(kind for kind, _ in items)
    shapes, scratch, specs, out_specs = ride_shapes(lax.axis_size(axis), items)
    samples, chans = signal.shape
    tile = DILATION_STEP
    steps, pools = samples // tile, tile // POOL
    block = pl.BlockSpec((tile, chans), lambda i: (i, 0))
    sums = pl.BlockSpec((1, pools, chans), lambda i: (i, 0, 0))
    gate = jax.ShapeDtypeStruct((samples, chans), F32)
    pooled = jax.ShapeDtypeStruct((steps, pools, chans), F32)
    return pl.pallas_call(
        functools.partial(forward_kernel, steps, axis, kinds),
        grid=(steps,),
        out_shape=[gate, gate, pooled, pooled] + shapes,
        in_specs=[
            pl.BlockSpec(memory_space=pltpu.SMEM),
            pl.BlockSpec((tile, chans), lambda i: (0, 0)),
            pl.BlockSpec((tile, chans), lambda i: (jnp.maximum(i - 1, 0), 0)),
            block,
            pl.BlockSpec(w_conv.shape, lambda i: (0, 0)),
        ]
        + specs,
        out_specs=[block, block, sums, sums] + out_specs,
        scratch_shapes=scratch,
        compiler_params=pltpu.CompilerParams(collective_id=collective, has_side_effects=True),
        name="conv_forward",
    )(info, incoming, signal, signal, w_conv, *[array for _, array in items])


def conv_backward(
    info, incoming, signal, t, s, d_hidden, d_resid, w_conv, axis, collective, items
):
    kinds = tuple(kind for kind, _ in items)
    shapes, scratch, specs, out_specs = ride_shapes(lax.axis_size(axis), items)
    samples, chans = signal.shape
    tile = DILATION_STEP
    steps, pools = samples // tile, tile // POOL
    block = pl.BlockSpec((tile, chans), lambda i: (steps - 1 - i, 0))
    fixed = pl.BlockSpec((tile, chans), lambda i: (0, 0))
    sums = pl.BlockSpec((1, pools, chans), lambda i: (steps - 1 - i, 0, 0))
    whole = pl.BlockSpec(w_conv.shape, lambda i: (0, 0))
    return pl.pallas_call(
        functools.partial(backward_kernel, steps, axis, kinds),
        grid=(steps,),
        out_shape=[
            jax.ShapeDtypeStruct((samples, chans), BF16),
            jax.ShapeDtypeStruct((tile, chans), BF16),
            jax.ShapeDtypeStruct(w_conv.shape, BF16),
        ]
        + shapes,
        in_specs=[
            pl.BlockSpec(memory_space=pltpu.SMEM),
            fixed,
            pl.BlockSpec((tile, chans), lambda i: (jnp.maximum(steps - 2 - i, 0), 0)),
            block,
            block,
            block,
            sums,
            sums,
            whole,
        ]
        + specs,
        out_specs=[block, fixed, whole] + out_specs,
        scratch_shapes=[pltpu.VMEM(w_conv.shape, F32), pltpu.VMEM((tile, chans), BF16)] + scratch,
        compiler_params=pltpu.CompilerParams(collective_id=collective, has_side_effects=True),
        name="conv_backward",
    )(info, incoming, signal, signal, t, s, d_hidden, d_resid, w_conv, *[a for _, a in items])


def shifted(value, axis, by):
    length = lax.axis_size(axis)
    pairs = [(i, i + by) for i in range(length) if 0 <= i + by < length]
    return lax.ppermute(value, axis, pairs)


def local(signal, lengths, w_conv, w_res, w_in, w_qkv, w_out, d_out):
    stays, samples, chans = signal.shape
    width = w_in.shape[1]
    size = width // HEADS
    heads = w_out.shape[0] // size
    toks = samples // POOL
    tms, parts = lax.axis_size("tm"), lax.axis_size("stream")
    tm = lax.axis_index("tm")
    group = stays * parts
    total = toks * tms
    flat = signal.reshape(samples, chans)
    incoming = shifted(flat[samples - DILATION_STEP :], "tm", 1)
    info = jnp.stack([tm * samples, lengths[0]]).astype(jnp.int32)
    lens8 = jnp.broadcast_to(lengths.reshape(stays, 1, 1), (stays, 8, 128))
    g_dout, g_len = exchange("stream", 0, [("gather", d_out), ("gather", lens8)])
    group_grad = g_dout.reshape(group, toks, width)
    group_len = g_len.reshape(group, 8, 128)[:, 0, 0]
    d_ctx = dot("btd,ed->bte", group_grad, w_out).astype(BF16)
    columns = width // tms
    grad_cols = group_grad.reshape(group, toks, tms, columns).transpose(2, 0, 1, 3)
    tanh_f, sig_g, h_sum, s_sum, all_ctx, all_cols = conv_forward(
        info, incoming, flat, w_conv, "tm", 6, [("gather1", d_ctx), ("scatter1", grad_cols)]
    )
    h_sum = h_sum.reshape(toks, chans)
    h_part = jnp.dot(h_sum, w_res.astype(F32), precision=HIGH)
    pooled = ((s_sum.reshape(toks, chans) + h_part) / POOL).astype(BF16)[None]
    own_tok = dot("btc,cd->btd", pooled, w_in).astype(BF16)
    (stay_pool,) = exchange("tm", 1, [("gather1", pooled)])
    (all_pool,) = exchange("stream", 7, [("gather", stay_pool.reshape(stays, total, chans))])
    all_pool = all_pool.reshape(group, total, chans)
    all_ctx = all_ctx.reshape(group, total, heads * size)
    all_cols = all_cols.reshape(group, total, columns)
    tok = dot("btc,cd->btd", all_pool, w_in).astype(BF16).astype(F32)
    r = lax.rsqrt(jnp.mean(tok * tok, axis=-1, keepdims=True) + EPS)
    normed = (tok * r).astype(BF16)
    proj = dot("btd,de->bte", normed, w_qkv).astype(BF16)
    context, d_proj = attention(proj, all_ctx, group_len, heads, size)
    own_ctx = lax.dynamic_slice_in_dim(context, tm * toks, toks, 1)
    out_part = dot("bte,ed->btd", own_ctx, w_out).astype(BF16)
    g_out = dot("bte,btd->ed", context, all_cols)
    own_norm = lax.dynamic_slice_in_dim(normed, tm * columns, columns, 2)
    g_qkv = dot("btd,bte->de", own_norm, d_proj)
    d_normed = dot("bte,de->btd", d_proj, w_qkv)
    inner = jnp.sum(d_normed * tok, axis=-1, keepdims=True)
    d_group = (r * d_normed - tok * (r * r * r) * inner / width).astype(BF16)
    own_group = lax.dynamic_slice_in_dim(d_group, tm * toks, toks, 1)
    g_in_part = dot("btc,btd->cd", all_pool, d_group).astype(BF16)
    in_rows = chans // parts
    g_in_cols = dot("btc,btd->cd", all_pool, all_cols)
    stream = lax.axis_index("stream")
    g_in_cols = lax.dynamic_slice_in_dim(g_in_cols, stream * in_rows, in_rows, 0)
    (s_group,) = exchange(
        "stream", 2, [("reduce", own_group.reshape(parts, stays, toks, width))]
    )
    d_tok = (s_group + d_out.astype(F32)).astype(BF16)
    d_pooled = dot("btd,cd->btc", d_tok, w_in)
    d_res16 = (d_pooled / POOL).astype(BF16).reshape(toks, chans)
    g_res = lax.dot_general(h_sum, d_res16.astype(F32), (((0,), (0,)), ((), ())), precision=HIGH)
    d_hidden = lax.dot_general(
        d_res16, w_res, (((1,), (1,)), ((), ())), preferred_element_type=F32
    )
    per_tile = (samples // DILATION_STEP, DILATION_STEP // POOL, chans)
    d_sig, first, g_conv, s_out, s_in = conv_backward(
        info,
        incoming,
        flat,
        tanh_f,
        sig_g,
        d_hidden.reshape(per_tile),
        d_res16.astype(F32).reshape(per_tile),
        w_conv,
        "stream",
        8,
        [
            ("reduce", out_part.reshape(parts, stays, toks, width)),
            ("reduce", g_in_part.reshape(parts, in_rows, width)),
        ],
    )
    out = (own_tok.astype(F32) + s_out).astype(BF16)
    arriving = shifted(first, "tm", -1)
    edge = samples - DILATION_STEP
    last = (d_sig[edge:].astype(F32) + arriving.astype(F32)).astype(BF16)
    d_signal = jnp.concatenate([d_sig[:edge], last], axis=0)[None]
    s_conv, s_res = exchange(
        "stream",
        3,
        [
            ("reduceb", g_conv.reshape(parts, -1, 2 * chans)),
            ("reduceb", g_res.astype(BF16).reshape(parts, -1, chans)),
        ],
    )
    a_conv, a_res, a_in = final_sums(
        "tm",
        4,
        s_conv.reshape(tms, -1, 2 * chans),
        s_res.reshape(tms, -1, chans),
        g_in_cols.astype(BF16),
    )
    sum_conv = a_conv.reshape(2 * chans // parts, 2 * chans).astype(F32)
    sum_res = a_res.reshape(chans // parts, chans).astype(F32)
    sum_in = s_in + a_in.transpose(1, 0, 2).reshape(in_rows, width).astype(F32)
    return (out, d_signal, sum_conv, sum_res, sum_in, g_qkv, g_out)


def solution(mesh):
    in_specs = (
        P("stream", "tm", None),
        P("stream"),
        P(),
        P(),
        P(),
        P(None, "stream"),
        P("stream", None),
        P("stream", "tm", None),
    )
    out_specs = (
        P("stream", "tm", None),
        P("stream", "tm", None),
        P("stream", None),
        P("stream", None),
        P("stream", None),
        P("tm", "stream"),
        P("stream", "tm"),
    )
    return jax.shard_map(local, mesh=mesh, in_specs=in_specs, out_specs=out_specs, check_vma=False)
```
